32 devices in a mesh: band: 8 (over z, x), cuts: 4 (over y, core).
Axes of the slice: x: 2, y: 2, z: 4, core: 2. Of those that a mesh axis runs over, the one named last changes fastest.
Arguments:
- var_feat: bfloat16 [163840, 128], P(('band', 'cuts')), may hold values from -6 to 6
- con_feat: bfloat16 [4096, 128], P(('band', 'cuts')), may hold values from -6 to 6
- slot_column_block: int32 [5120], P(('band', 'cuts')), may hold values from 0 to 39
- slot_constraint_block: int32 [5120], P(('band', 'cuts')), may hold values from 0 to 7
- block_count: int32 [32], P(('band', 'cuts')), may hold values from 40 to 160, as said below
- incidence_coefficients: int32 [5120, 128, 128], P(('band', 'cuts')), may hold values from -3 to 4
- con_first: bfloat16 [256, 256], replicated, may hold values from -0.375 to 0.375
- con_bias: float32 [256], replicated, may hold values from -3 to 3
- con_second: bfloat16 [256, 256], replicated, may hold values from -0.375 to 0.375
- con_third: bfloat16 [256, 128], replicated, may hold values from -0.375 to 0.375
- con_gain: float32 [128], replicated, may hold values from 0.1 to 1.9
- con_shift: float32 [128], replicated, may hold values from -3 to 3
- var_first: bfloat16 [256, 256], replicated, may hold values from -0.375 to 0.375
- var_bias: float32 [256], replicated, may hold values from -3 to 3
- var_second: bfloat16 [256, 256], replicated, may hold values from -0.375 to 0.375
- var_third: bfloat16 [256, 128], replicated, may hold values from -0.375 to 0.375
- var_gain: float32 [128], replicated, may hold values from 0.1 to 1.9
- var_shift: float32 [128], replicated, may hold values from -3 to 3
Outputs:
- con_new: bfloat16 [4096, 128], P(('band', 'cuts'))
- var_new: bfloat16 [163840, 128], P(('band', 'cuts'))
The draws below stay inside these ranges and needn't reach their ends.
Inputs may be any that keep to these rules, and one draw needn't show every extreme that they name: Each device's live slots are its first block_count slots; in every draw one eighth of the devices hold 160 live slots and some device holds 40.
All inputs are finite; a program needn't handle non-finite values.
Results may differ from the reference program's by a relative error of at most 0.0075.
Values may be sent and summed in bfloat16 or wider, within the bound.
A program may use at most 128 MiB of HBM per device.

```python
import math
import jax
import jax.numpy as jnp
from jax import lax

W = 128
HID = 256
INCIDENCE_ORDER = 128
CONSTRAINT_BLKS = 1
PATTERN_BLOCKS = 40
NB = 160
NV = 163840
NC = 4096
TOTAL_SLOTS = 5120
N_BAND = 8
N_CUTS = 4


def draw_block_count(key, part):
    device_total = N_BAND * N_CUTS
    first_key, second_key = jax.random.split(key)
    live_slots = PATTERN_BLOCKS + jax.random.randint(first_key, (device_total,), 0, PATTERN_BLOCKS + 1)
    shuffled = jax.random.permutation(second_key, device_total)
    full_rank = jnp.zeros((device_total,), jnp.int32).at[shuffled].set(jnp.arange(device_total, dtype=jnp.int32))
    heavy = full_rank < device_total // 8
    live_slots = jnp.where(heavy, 4 * PATTERN_BLOCKS, live_slots)
    live_slots = jnp.where(full_rank == device_total - 1, PATTERN_BLOCKS, live_slots)
    return live_slots.astype(jnp.int32)


def plant(result, key, least, top_value):
    shape = result.shape
    spot = [jax.random.randint(jax.random.fold_in(key, axis), (), 0, shape[axis]) for axis in range(len(shape))]
    result = result.at[tuple(spot)].set(least)
    longest = shape.index(max(shape))
    spot[longest] = (spot[longest] + 1) % shape[longest]
    return result.at[tuple(spot)].set(top_value)


def levels(rng, extent, cuts, low, largest):
    level = 1.0
    for axis_at, parts in cuts:
        heights = jax.random.uniform(jax.random.fold_in(jax.random.fold_in(rng, 6), axis_at), (parts,), jnp.float32, low / len(cuts), largest / len(cuts))
        level = level * jnp.repeat(jnp.exp(heights), extent[axis_at] // parts).reshape((-1,) + (1,) * (len(extent) - 1 - axis_at))
    return level


def scatter_about(rng, extent, scale, bound, shards=(), kind=jnp.bfloat16):
    entries = scale * jax.random.normal(rng, extent, jnp.float32)
    if shards:
        entries = entries * levels(rng, extent, shards, -0.22, 0.18)
    return jnp.clip(entries, -bound, bound).astype(kind)


def setup_inputs(seed: int = 0) -> dict:
    seeds = jax.random.split(jax.random.key(seed), 19)
    var_feat = scatter_about(seeds[0], (NV, W), 1.0, 6.0, ((0, 32),))
    con_feat = scatter_about(seeds[1], (NC, W), 1.0, 6.0, ((0, 32),))
    slot_column_block = plant(jax.random.randint(seeds[2], (TOTAL_SLOTS,), 0, PATTERN_BLOCKS), jax.random.fold_in(seeds[2], 1), 0, PATTERN_BLOCKS - 1).astype(jnp.int32)
    slot_constraint_block = plant(jax.random.randint(seeds[3], (TOTAL_SLOTS,), 0, 2 * CONSTRAINT_BLKS * N_CUTS), jax.random.fold_in(seeds[3], 1), 0, (2 * CONSTRAINT_BLKS * N_CUTS) - 1).astype(jnp.int32)
    block_count = draw_block_count(jax.random.fold_in(seeds[18], 71), 0)
    incidence_coefficients = plant(jax.random.randint(seeds[5], (TOTAL_SLOTS, INCIDENCE_ORDER, INCIDENCE_ORDER), -3, 5), jax.random.fold_in(seeds[5], 1), -3, 4).astype(jnp.int32)
    con_first = scatter_about(seeds[6], (2 * W, HID), (2 * W) ** -0.5, 0.375)
    con_bias = scatter_about(seeds[7], (HID,), 0.5, 3.0, (), jnp.float32)
    con_second = scatter_about(seeds[8], (HID, HID), HID ** -0.5, 0.375)
    con_third = scatter_about(seeds[9], (HID, W), HID ** -0.5, 0.375)
    con_gain = jnp.clip(1.0 + 0.18 * jax.random.normal(seeds[10], (W,), jnp.float32), 0.1, 1.9)
    con_shift = scatter_about(seeds[11], (W,), 0.5, 3.0, (), jnp.float32)
    var_first = scatter_about(seeds[12], (2 * W, HID), (2 * W) ** -0.5, 0.375)
    var_bias = scatter_about(seeds[13], (HID,), 0.5, 3.0, (), jnp.float32)
    var_second = scatter_about(seeds[14], (HID, HID), HID ** -0.5, 0.375)
    var_third = scatter_about(seeds[15], (HID, W), HID ** -0.5, 0.375)
    var_gain = jnp.clip(1.0 + 0.18 * jax.random.normal(seeds[16], (W,), jnp.float32), 0.1, 1.9)
    var_shift = scatter_about(seeds[17], (W,), 0.5, 3.0, (), jnp.float32)
    return {"var_feat": var_feat, "con_feat": con_feat, "slot_column_block": slot_column_block, "slot_constraint_block": slot_constraint_block, "block_count": block_count, "incidence_coefficients": incidence_coefficients, "con_first": con_first, "con_bias": con_bias, "con_second": con_second, "con_third": con_third, "con_gain": con_gain, "con_shift": con_shift, "var_first": var_first, "var_bias": var_bias, "var_second": var_second, "var_third": var_third, "var_gain": var_gain, "var_shift": var_shift}


EPS = 1e-05

def layer_norm(values, gain, offset):
    center = values - lax.optimization_barrier(jnp.mean(values, axis=-1, keepdims=True))
    spread = lax.optimization_barrier(jnp.mean(center * center, axis=-1, keepdims=True))
    return center * lax.rsqrt(spread + EPS) * gain + offset

def node_update(feats, scaled_agg, w_first, bias, w_second, w_third, gain, offset):
    joined = jnp.concatenate([feats, scaled_agg.astype(jnp.bfloat16)], axis=1)
    hidden = jnp.maximum(jnp.dot(joined, w_first, preferred_element_type=jnp.float32) + bias, 0.0).astype(jnp.bfloat16)
    middle = jnp.maximum(jnp.dot(hidden, w_second, preferred_element_type=jnp.float32), 0.0).astype(jnp.bfloat16)
    output = jnp.dot(middle, w_third, preferred_element_type=jnp.float32)
    return layer_norm(feats.astype(jnp.float32) + output, gain, offset).astype(jnp.bfloat16)

def reference(var_feat, con_feat, slot_column_block, slot_constraint_block, block_count, incidence_coefficients, con_first, con_bias, con_second, con_third, con_gain, con_shift, var_first, var_bias, var_second, var_third, var_gain, var_shift):
    device_total = N_BAND * N_CUTS
    band_blocks = CONSTRAINT_BLKS * N_CUTS
    band_rows = band_blocks * INCIDENCE_ORDER
    width = var_feat.shape[1]
    var_blocks = var_feat.reshape(device_total, PATTERN_BLOCKS, INCIDENCE_ORDER, width)
    col_index = slot_column_block.reshape(device_total, NB)
    row_index = slot_constraint_block.reshape(device_total, NB)
    coef_all = incidence_coefficients.reshape(device_total, NB, INCIDENCE_ORDER, INCIDENCE_ORDER)
    slot_ids = jnp.arange(NB, dtype=jnp.int32)
    row_ids = jnp.arange(2 * band_blocks, dtype=jnp.int32)
    col_ids = jnp.arange(PATTERN_BLOCKS, dtype=jnp.int32)
    highest = lax.Precision.HIGHEST

    def accumulate(carry, device):
        live = (slot_ids < block_count[device]).astype(jnp.float32)
        picked = jnp.take(var_blocks[device], col_index[device], axis=0).astype(jnp.float32)
        coef = coef_all[device].astype(jnp.float32)
        products = jnp.einsum('sij,sjw->siw', coef, picked, precision=highest)
        selector = (row_index[device][None, :] == row_ids[:, None]).astype(jnp.float32) * live[None, :]
        term = jnp.einsum('rs,siw->riw', selector, products, precision=highest).reshape(2 * band_rows, width)
        start = device // N_CUTS * band_rows
        current = lax.dynamic_slice_in_dim(carry, start, 2 * band_rows, 0)
        return (lax.dynamic_update_slice_in_dim(carry, current + term, start, 0), None)
    padded = jnp.zeros((NC + band_rows, width), jnp.float32)
    con_agg, _ = lax.scan(accumulate, padded, jnp.arange(device_total, dtype=jnp.int32))
    con_agg = con_agg[:NC] * (1.0 / math.sqrt(INCIDENCE_ORDER * NB))
    con_new = node_update(con_feat, con_agg, con_first, con_bias, con_second, con_third, con_gain, con_shift)
    con_padded = jnp.concatenate([con_new, jnp.zeros((band_rows, width), jnp.bfloat16)], axis=0)

    def update(device):
        live = (slot_ids < block_count[device]).astype(jnp.float32)
        start = device // N_CUTS * band_rows
        window = lax.dynamic_slice_in_dim(con_padded, start, 2 * band_rows, 0).reshape(2 * band_blocks, INCIDENCE_ORDER, width)
        picked = jnp.take(window, row_index[device], axis=0).astype(jnp.float32)
        coef = coef_all[device].astype(jnp.float32)
        products = jnp.einsum('sij,siw->sjw', coef, picked, precision=highest)
        selector = (col_index[device][None, :] == col_ids[:, None]).astype(jnp.float32) * live[None, :]
        var_agg = jnp.einsum('cs,sjw->cjw', selector, products, precision=highest).reshape(PATTERN_BLOCKS * INCIDENCE_ORDER, width)
        var_agg = var_agg * (1.0 / math.sqrt(4 * INCIDENCE_ORDER))
        own_feat = var_blocks[device].reshape(PATTERN_BLOCKS * INCIDENCE_ORDER, width)
        return node_update(own_feat, var_agg, var_first, var_bias, var_second, var_third, var_gain, var_shift)
    var_new = lax.map(update, jnp.arange(device_total, dtype=jnp.int32)).reshape(NV, width)
    return (con_new, var_new)
```

```python
import functools
import math

import jax
import jax.numpy as jnp
from jax import lax
from jax.experimental import pallas as pl
from jax.experimental.pallas import tpu as pltpu
from jax.sharding import PartitionSpec as P

EPS = 1e-05
F32 = jnp.float32
BF16 = jnp.bfloat16
MESH = pl.DeviceIdType.MESH
CHUNK = 16
UNROLL = 8


def layer_norm(values, gain, offset):
    center = values - jnp.mean(values, axis=-1, keepdims=True)
    spread = jnp.mean(center * center, axis=-1, keepdims=True)
    return center * lax.rsqrt(spread + EPS) * gain + offset


def node_update(feats, scaled_agg, w_first, bias, w_second, w_third, gain, offset):
    joined = jnp.concatenate([feats, scaled_agg.astype(BF16)], axis=1)
    hidden = jnp.maximum(jnp.dot(joined, w_first, preferred_element_type=F32) + bias, 0.0).astype(BF16)
    middle = jnp.maximum(jnp.dot(hidden, w_second, preferred_element_type=F32), 0.0).astype(BF16)
    output = jnp.dot(middle, w_third, preferred_element_type=F32)
    return layer_norm(feats.astype(F32) + output, gain, offset).astype(BF16)


def order_rows(key_row, key_col, other_col, live_row, live_col, lanes, group):
    slots = key_col.shape[0]
    iota = lambda shape, axis: lax.broadcasted_iota(jnp.int32, shape, axis)
    lane = iota((slots, lanes), 1)
    before = (key_row == key_col) & (iota((slots, slots), 1) < iota((slots, slots), 0))
    within = jnp.sum(jnp.where(before, live_row, 0), axis=1, keepdims=True)
    counts = jnp.sum(jnp.where(lane == key_col, live_col, 0), axis=0, keepdims=True)
    counts_col = jnp.sum(jnp.where(iota((lanes, slots), 0) == key_row, live_row, 0), axis=1, keepdims=True)
    steps, steps_col = counts, counts_col
    if group == 2:
        steps, steps_col = (counts + 1) >> 1, (counts_col + 1) >> 1
    base_col = jnp.sum(jnp.where(lane < key_col, steps, 0), axis=1, keepdims=True)
    place = jnp.where(live_col > 0, base_col * group + within, -1)
    hit = place == lane
    index = jnp.sum(jnp.where(hit, iota((slots, lanes), 0) - slots, 0), axis=0, keepdims=True) + slots
    other = jnp.sum(jnp.where(hit, other_col, 0), axis=0, keepdims=True)
    opens = (place == lane * group) & (within == 0)
    carry = 1 - jnp.sum(jnp.where(opens, 1, 0), axis=0, keepdims=True)
    upto = iota((lanes, lanes), 0) <= iota((lanes, lanes), 1)
    ends = jnp.sum(jnp.where(upto, steps_col, 0), axis=0, keepdims=True)
    last = jnp.maximum(ends - 1, 0)
    filled = jnp.where(counts > 0, 1, 0)
    return [index, other, carry, last, filled]


def kernel(
    dims,
    cb_s, rb_s, cb_v, rb_v, count_s,
    vf_hbm, cf, coef_hbm,
    cw1, cbias, cw2, cw3, cgain, cshift,
    vw1, vbias, vw2, vw3, vgain, vshift,
    con_out, var_out,
    raw, half, prod, scan, paired, feat, result, part, arrive, window, conbuf,
    order_v, order_s,
    raw_sem, feat_sem, order_sem, out_sem, psend, precv, wsend, wrecv,
):
    nb, nc, slots, size, cols, pairs, lanes, chunks = dims
    band = lax.axis_index("band")
    cut = lax.axis_index("cuts")
    has_next = band < nb - 1
    has_prev = band > 0

    feat_copy = pltpu.make_async_copy(vf_hbm, feat, feat_sem)
    feat_copy.start()

    def raw_copy(i):
        piece = pl.ds(i * CHUNK, CHUNK)
        return pltpu.make_async_copy(coef_hbm.at[piece], raw.at[piece], raw_sem.at[i])

    for i in range(chunks):
        raw_copy(i).start()

    barrier = pltpu.get_barrier_semaphore()
    for d in range(1, nc):
        pl.semaphore_signal(barrier, inc=1, device_id=(band, lax.rem(cut + d, nc)), device_id_type=MESH)

    @pl.when(has_next)
    def _():
        for d in range(nc):
            pl.semaphore_signal(barrier, inc=1, device_id=(band + 1, lax.rem(cut + d, nc)), device_id_type=MESH)

    @pl.when(has_prev)
    def _():
        for d in range(nc):
            pl.semaphore_signal(barrier, inc=1, device_id=(band - 1, lax.rem(cut + d, nc)), device_id_type=MESH)

    row_c = cb_v[...]
    row_r = rb_v[...]
    diagonal = lax.broadcasted_iota(jnp.int32, (slots, slots), 0) == lax.broadcasted_iota(jnp.int32, (slots, slots), 1)
    col_c = jnp.sum(jnp.where(diagonal, row_c, 0), axis=1, keepdims=True)
    col_r = jnp.sum(jnp.where(diagonal, row_r, 0), axis=1, keepdims=True)
    count = count_s[0]
    live_row = jnp.where(lax.broadcasted_iota(jnp.int32, (1, slots), 1) < count, 1, 0)
    live_col = jnp.where(lax.broadcasted_iota(jnp.int32, (slots, 1), 0) < count, 1, 0)
    rows = order_rows(row_r, col_r, col_c, live_row, live_col, lanes, 1)
    rows += order_rows(row_c, col_c, col_r, live_row, live_col, lanes, 2)
    rows += [jnp.zeros((1, lanes), jnp.int32)] * (16 - len(rows))
    order_v[...] = jnp.concatenate(rows, axis=0)
    order_copy = pltpu.make_async_copy(order_v, order_s, order_sem)
    order_copy.start()

    half[slots] = jnp.zeros((size, size), BF16)
    prod[slots] = jnp.zeros((size, prod.shape[2]), F32)

    @pl.when(jnp.logical_not(has_prev))
    def _():
        arrive[pl.ds(nc, nc)] = jnp.zeros((nc,) + arrive.shape[1:], BF16)

    @pl.when(jnp.logical_not(has_next))
    def _():
        window[pl.ds(nc, nc)] = jnp.zeros((nc,) + window.shape[1:], BF16)

    feat_copy.wait()

    def forward(i, _):
        raw_copy(i).wait()

        def some(j, _):
            for u in range(UNROLL):
                s = i * CHUNK + j * UNROLL + u
                a = raw[s].astype(F32).astype(BF16)
                half[s] = a
                prod[s] = jnp.dot(a, feat[cb_s[s]], preferred_element_type=F32)
            return 0

        lax.fori_loop(0, CHUNK // UNROLL, some, 0)
        return 0

    lax.fori_loop(0, chunks, forward, 0)
    order_copy.wait()

    def sum_slots(k, carry):
        for u in range(4):
            at = k * 4 + u
            carry = carry * order_s[2, at].astype(F32) + prod[order_s[0, at]]
            scan[at] = carry
        return carry

    lax.fori_loop(0, slots // 4, sum_slots, jnp.zeros(prod.shape[1:], F32))

    blocks = part.shape[1] // size

    def fill(q):
        for e in range(blocks):
            r = q * blocks + e
            part[q, e * size : (e + 1) * size] = (scan[order_s[3, r]] * order_s[4, r].astype(F32)).astype(BF16)

    def part_send(d, ahead):
        to = lax.rem(cut + d, nc)
        q = ahead * nc + d
        return pltpu.make_async_remote_copy(
            src_ref=part.at[ahead * nc + to], dst_ref=arrive.at[ahead * nc + cut],
            send_sem=psend.at[q], recv_sem=precv.at[ahead * nc + cut],
            device_id=(band + ahead, to), device_id_type=MESH)

    def part_wait(src, ahead):
        pltpu.make_async_remote_copy(
            src_ref=part.at[0], dst_ref=arrive.at[ahead * nc + src],
            send_sem=psend.at[0], recv_sem=precv.at[ahead * nc + src],
            device_id=(band, cut), device_id_type=MESH).wait_recv()

    for q in range(2 * nc):
        fill(q)

    expected = (nc - 1) + jnp.where(has_next, nc, 0) + jnp.where(has_prev, nc, 0)
    pl.semaphore_wait(barrier, expected)

    @pl.when(has_next)
    def _():
        for d in range(nc):
            part_send(d, 1).start()

    for d in range(1, nc):
        part_send(d, 0).start()

    def pair_up(p, _):
        for u in range(2):
            k = p * 2 + u
            left = half[order_s[5, 2 * k]].T
            right = half[order_s[5, 2 * k + 1]].T
            paired[k, :, :size] = left
            paired[k, :, size:] = right
        return 0

    lax.fori_loop(0, pairs // 4, pair_up, 0)

    total = part[cut].astype(F32)
    for d in range(1, nc):
        src = lax.rem(cut + d, nc)
        part_wait(src, 0)
        total += arrive[src].astype(F32)

    @pl.when(has_prev)
    def _():
        for src in range(nc):
            part_wait(src, 1)

    for src in range(nc):
        total += arrive[nc + src].astype(F32)

    con_new = node_update(
        cf[...], total * (1.0 / math.sqrt(size * slots)), cw1[...], cbias[...], cw2[...], cw3[...], cgain[...], cshift[...])
    conbuf[...] = con_new
    con_out[...] = con_new
    window[cut] = con_new

    def win_send(d, back):
        to = lax.rem(cut + d, nc)
        return pltpu.make_async_remote_copy(
            src_ref=conbuf, dst_ref=window.at[back * nc + cut],
            send_sem=wsend.at[back * nc + d], recv_sem=wrecv.at[back * nc + cut],
            device_id=(band - back, to), device_id_type=MESH)

    def win_wait(src, back):
        pltpu.make_async_remote_copy(
            src_ref=conbuf, dst_ref=window.at[back * nc + src],
            send_sem=wsend.at[0], recv_sem=wrecv.at[back * nc + src],
            device_id=(band, cut), device_id_type=MESH).wait_recv()

    @pl.when(has_prev)
    def _():
        for d in range(nc):
            win_send(d, 1).start()

    for d in range(1, nc):
        win_send(d, 0).start()

    lax.fori_loop(pairs // 4, pairs // 2, pair_up, 0)

    @pl.when(has_next)
    def _():
        for d in range(nc):
            part_send(d, 1).wait_send()

    for d in range(1, nc):
        part_send(d, 0).wait_send()
        win_wait(lax.rem(cut + d, nc), 0)

    @pl.when(has_next)
    def _():
        for src in range(nc):
            win_wait(src, 1)

    def row_block(r):
        if blocks == 1:
            return window[r]
        return window[r // blocks, pl.ds(pl.multiple_of(r % blocks * size, size), size)]

    def back(k, carry):
        for u in range(4):
            at = k * 4 + u
            right = jnp.concatenate([row_block(order_s[6, 2 * at]), row_block(order_s[6, 2 * at + 1])], axis=0)
            term = jnp.dot(paired[at], right, preferred_element_type=F32)
            carry = carry * order_s[7, at].astype(F32) + term
            scan[at] = carry
        return carry

    lax.fori_loop(0, pairs // 4, back, jnp.zeros(scan.shape[1:], F32))

    scale = 1.0 / math.sqrt(4 * size)
    w1, w2, w3 = vw1[...], vw2[...], vw3[...]
    bias, gain, shift = vbias[...], vgain[...], vshift[...]

    def out_copy(i):
        piece = pl.ds(i * 2, 2)
        return pltpu.make_async_copy(result.at[piece], var_out.at[piece], out_sem.at[i])

    def update(i, _):
        feats, aggs = [], []
        for u in range(2):
            c = i * 2 + u
            feats.append(feat[c])
            aggs.append(scan[order_s[8, c]] * (order_s[9, c].astype(F32) * scale))
        new = node_update(
            jnp.concatenate(feats, axis=0), jnp.concatenate(aggs, axis=0), w1, bias, w2, w3, gain, shift)
        result[i * 2] = new[:size]
        result[i * 2 + 1] = new[size:]
        out_copy(i).start()
        return 0

    lax.fori_loop(0, cols // 2, update, 0)

    @pl.when(has_prev)
    def _():
        for d in range(nc):
            win_send(d, 1).wait_send()

    for d in range(1, nc):
        win_send(d, 0).wait_send()

    def finish(i, _):
        out_copy(i).wait()
        return 0

    lax.fori_loop(0, cols // 2, finish, 0)


def on_device(
    nb, nc,
    var_feat, con_feat, slot_column_block, slot_constraint_block, block_count, incidence_coefficients,
    con_first, con_bias, con_second, con_third, con_gain, con_shift,
    var_first, var_bias, var_second, var_third, var_gain, var_shift,
):
    width = var_feat.shape[1]
    slots = slot_column_block.shape[0]
    size = incidence_coefficients.shape[1]
    cols = var_feat.shape[0] // size
    rows = con_feat.shape[0]
    pairs = -(-(slots + cols) // 8) * 4
    lanes = -(-max(2 * pairs, slots) // 128) * 128
    chunks = slots // CHUNK
    dims = (nb, nc, slots, size, cols, pairs, lanes, chunks)
    smem = pl.BlockSpec(memory_space=pltpu.SMEM)
    vmem = pl.BlockSpec(memory_space=pltpu.VMEM)
    hbm = pl.BlockSpec(memory_space=pl.ANY)
    row = lambda v: v.reshape(1, -1)
    con_new, var_new = pl.pallas_call(
        functools.partial(kernel, dims),
        out_shape=(
            jax.ShapeDtypeStruct(con_feat.shape, BF16),
            jax.ShapeDtypeStruct((cols, size, width), BF16),
        ),
        in_specs=[smem, smem, vmem, vmem, smem, hbm, vmem, hbm] + [vmem] * 12,
        out_specs=(vmem, hbm),
        scratch_shapes=[
            pltpu.VMEM((slots, size, size), jnp.int32),
            pltpu.VMEM((slots + 1, size, size), BF16),
            pltpu.VMEM((slots + 1, size, width), F32),
            pltpu.VMEM((max(slots, pairs), size, width), F32),
            pltpu.VMEM((pairs, size, 2 * size), BF16),
            pltpu.VMEM((cols, size, width), BF16),
            pltpu.VMEM((cols, size, width), BF16),
            pltpu.VMEM((2 * nc, rows, width), BF16),
            pltpu.VMEM((2 * nc, rows, width), BF16),
            pltpu.VMEM((2 * nc, rows, width), BF16),
            pltpu.VMEM((rows, width), BF16),
            pltpu.VMEM((16, lanes), jnp.int32),
            pltpu.SMEM((16, lanes), jnp.int32),
            pltpu.SemaphoreType.DMA((chunks,)),
            pltpu.SemaphoreType.DMA,
            pltpu.SemaphoreType.DMA,
            pltpu.SemaphoreType.DMA((cols // 2,)),
            pltpu.SemaphoreType.DMA((2 * nc,)),
            pltpu.SemaphoreType.DMA((2 * nc,)),
            pltpu.SemaphoreType.DMA((2 * nc,)),
            pltpu.SemaphoreType.DMA((2 * nc,)),
        ],
        compiler_params=pltpu.CompilerParams(
            collective_id=0, has_side_effects=True, vmem_limit_bytes=63 * 1024 * 1024),
        name="layer",
    )(
        slot_column_block, slot_constraint_block, row(slot_column_block), row(slot_constraint_block), block_count,
        var_feat.reshape(cols, size, width), con_feat, incidence_coefficients,
        con_first, row(con_bias), con_second, con_third, row(con_gain), row(con_shift),
        var_first, row(var_bias), var_second, var_third, row(var_gain), row(var_shift),
    )
    return con_new, var_new.reshape(var_feat.shape)


def solution(mesh):
    both = P(("band", "cuts"))
    wide = P(("band", "cuts"), None)
    in_specs = (wide, wide, both, both, both, P(("band", "cuts"), None, None)) + (P(),) * 12
    body = functools.partial(on_device, mesh.shape["band"], mesh.shape["cuts"])
    return jax.shard_map(body, mesh=mesh, in_specs=in_specs, out_specs=(wide, wide), check_vma=False)
```

```python
import functools
import math

import jax
import jax.numpy as jnp
from jax import lax
from jax.experimental import pallas as pl
from jax.experimental.pallas import tpu as pltpu
from jax.sharding import PartitionSpec as P

EPS = 1e-05
F32 = jnp.float32
BF16 = jnp.bfloat16
MESH = pl.DeviceIdType.MESH
CHUNK = 16
UNROLL = 8
FORWARD = 12
BACK = 20
STEP = 8


def layer_norm(values, gain, offset):
    center = values - jnp.mean(values, axis=-1, keepdims=True)
    spread = jnp.mean(center * center, axis=-1, keepdims=True)
    return center * lax.rsqrt(spread + EPS) * gain + offset


def node_update(feats, scaled_agg, w_first, bias, w_second, w_third, gain, offset):
    joined = jnp.concatenate([feats, scaled_agg.astype(BF16)], axis=1)
    hidden = jnp.maximum(jnp.dot(joined, w_first, preferred_element_type=F32) + bias, 0.0).astype(BF16)
    middle = jnp.maximum(jnp.dot(hidden, w_second, preferred_element_type=F32), 0.0).astype(BF16)
    output = jnp.dot(middle, w_third, preferred_element_type=F32)
    return layer_norm(feats.astype(F32) + output, gain, offset).astype(BF16)


def order_rows(key_row, key_col, other_col, live_row, live_col, lanes, group):
    slots = key_col.shape[0]
    iota = lambda shape, axis: lax.broadcasted_iota(jnp.int32, shape, axis)
    lane = iota((slots, lanes), 1)
    before = (key_row == key_col) & (iota((slots, slots), 1) < iota((slots, slots), 0))
    within = jnp.sum(jnp.where(before, live_row, 0), axis=1, keepdims=True)
    counts = jnp.sum(jnp.where(lane == key_col, live_col, 0), axis=0, keepdims=True)
    counts_col = jnp.sum(jnp.where(iota((lanes, slots), 0) == key_row, live_row, 0), axis=1, keepdims=True)
    steps, steps_col = counts, counts_col
    if group == 2:
        steps, steps_col = (counts + 1) >> 1, (counts_col + 1) >> 1
    base_col = jnp.sum(jnp.where(lane < key_col, steps, 0), axis=1, keepdims=True)
    place = jnp.where(live_col > 0, base_col * group + within, -1)
    hit = place == lane
    index = jnp.sum(jnp.where(hit, iota((slots, lanes), 0) - slots, 0), axis=0, keepdims=True) + slots
    other = jnp.sum(jnp.where(hit, other_col, 0), axis=0, keepdims=True)
    opens = (place == lane * group) & (within == 0)
    carry = 1 - jnp.sum(jnp.where(opens, 1, 0), axis=0, keepdims=True)
    upto = iota((lanes, lanes), 0) <= iota((lanes, lanes), 1)
    ends = jnp.sum(jnp.where(upto, steps_col, 0), axis=0, keepdims=True)
    last = jnp.maximum(ends - 1, 0)
    filled = jnp.where(counts > 0, 1, 0)
    return [index, other, carry, last, filled]


def kernel(
    dims,
    cb_s, rb_s, cb_v, rb_v, count_s,
    vf_hbm, cf, coef_hbm,
    cw1, cbias, cw2, cw3, cgain, cshift,
    vw1, vbias, vw2, vw3, vgain, vshift,
    con_out, var_out,
    raw, half, scan, paired, feat, result, part, arrive, window, conbuf,
    order_v, order_s,
    raw_sem, feat_sem, order_sem, out_sem, psend, precv, wsend, wrecv,
):
    nb, nc, slots, size, cols, fpairs, pairs, lanes, chunks = dims
    band = lax.axis_index("band")
    cut = lax.axis_index("cuts")
    has_next = band < nb - 1
    has_prev = band > 0

    feat_copy = pltpu.make_async_copy(vf_hbm, feat, feat_sem)
    feat_copy.start()

    def raw_copy(i):
        piece = pl.ds(i * CHUNK, CHUNK)
        return pltpu.make_async_copy(coef_hbm.at[piece], raw.at[piece], raw_sem.at[i])

    for i in range(chunks):
        raw_copy(i).start()

    barrier = pltpu.get_barrier_semaphore()
    for d in range(1, nc):
        pl.semaphore_signal(barrier, inc=1, device_id=(band, lax.rem(cut + d, nc)), device_id_type=MESH)

    @pl.when(has_next)
    def _():
        for d in range(nc):
            pl.semaphore_signal(barrier, inc=1, device_id=(band + 1, lax.rem(cut + d, nc)), device_id_type=MESH)

    @pl.when(has_prev)
    def _():
        for d in range(nc):
            pl.semaphore_signal(barrier, inc=1, device_id=(band - 1, lax.rem(cut + d, nc)), device_id_type=MESH)

    row_c = cb_v[...]
    row_r = rb_v[...]
    diagonal = lax.broadcasted_iota(jnp.int32, (slots, slots), 0) == lax.broadcasted_iota(jnp.int32, (slots, slots), 1)
    col_c = jnp.sum(jnp.where(diagonal, row_c, 0), axis=1, keepdims=True)
    col_r = jnp.sum(jnp.where(diagonal, row_r, 0), axis=1, keepdims=True)
    count = count_s[0]
    live_row = jnp.where(lax.broadcasted_iota(jnp.int32, (1, slots), 1) < count, 1, 0)
    live_col = jnp.where(lax.broadcasted_iota(jnp.int32, (slots, 1), 0) < count, 1, 0)
    rows = order_rows(row_r, col_r, col_c, live_row, live_col, lanes, 2)
    rows += order_rows(row_c, col_c, col_r, live_row, live_col, lanes, 2)
    rows += [jnp.zeros((1, lanes), jnp.int32)] * (16 - len(rows))
    order_v[...] = jnp.concatenate(rows, axis=0)
    order_copy = pltpu.make_async_copy(order_v, order_s, order_sem)
    order_copy.start()

    half[slots] = jnp.zeros((size, size), BF16)

    @pl.when(jnp.logical_not(has_prev))
    def _():
        arrive[pl.ds(nc, nc)] = jnp.zeros((nc,) + arrive.shape[1:], BF16)

    @pl.when(jnp.logical_not(has_next))
    def _():
        window[pl.ds(nc, nc)] = jnp.zeros((nc,) + window.shape[1:], BF16)

    def convert(i, _):
        raw_copy(i).wait()

        def some(j, _):
            for u in range(UNROLL):
                at = i * CHUNK + j * UNROLL + u
                half[at] = raw[at].astype(F32).astype(BF16)
            return 0

        lax.fori_loop(0, CHUNK // UNROLL, some, 0)
        return 0

    lax.fori_loop(0, chunks, convert, 0)
    feat_copy.wait()
    order_copy.wait()

    def forward(k, carry):
        for u in range(FORWARD):
            at = k * FORWARD + u
            left = jnp.concatenate([half[order_s[0, 2 * at]], half[order_s[0, 2 * at + 1]]], axis=1)
            right = jnp.concatenate([feat[order_s[1, 2 * at]], feat[order_s[1, 2 * at + 1]]], axis=0)
            term = jnp.dot(left, right, preferred_element_type=F32)
            carry = carry * order_s[2, at].astype(F32) + term
            scan[at] = carry
        return carry

    lax.fori_loop(0, fpairs // FORWARD, forward, jnp.zeros(scan.shape[1:], F32))

    blocks = part.shape[1] // size

    def fill(q):
        for e in range(blocks):
            r = q * blocks + e
            part[q, e * size : (e + 1) * size] = (scan[order_s[3, r]] * order_s[4, r].astype(F32)).astype(BF16)

    def part_send(d, ahead):
        to = lax.rem(cut + d, nc)
        q = ahead * nc + d
        return pltpu.make_async_remote_copy(
            src_ref=part.at[ahead * nc + to], dst_ref=arrive.at[ahead * nc + cut],
            send_sem=psend.at[q], recv_sem=precv.at[ahead * nc + cut],
            device_id=(band + ahead, to), device_id_type=MESH)

    def part_wait(src, ahead):
        pltpu.make_async_remote_copy(
            src_ref=part.at[0], dst_ref=arrive.at[ahead * nc + src],
            send_sem=psend.at[0], recv_sem=precv.at[ahead * nc + src],
            device_id=(band, cut), device_id_type=MESH).wait_recv()

    for q in range(2 * nc):
        fill(q)

    expected = (nc - 1) + jnp.where(has_next, nc, 0) + jnp.where(has_prev, nc, 0)
    pl.semaphore_wait(barrier, expected)

    @pl.when(has_next)
    def _():
        for d in range(nc):
            part_send(d, 1).start()

    for d in range(1, nc):
        part_send(d, 0).start()

    def pair_up(p, _):
        for u in range(2):
            k = p * 2 + u
            left = half[order_s[5, 2 * k]].T
            right = half[order_s[5, 2 * k + 1]].T
            paired[k, :, :size] = left
            paired[k, :, size:] = right
        return 0

    lax.fori_loop(0, pairs // 4, pair_up, 0)

    total = part[cut].astype(F32)
    for d in range(1, nc):
        src = lax.rem(cut + d, nc)
        part_wait(src, 0)
        total += arrive[src].astype(F32)

    @pl.when(has_prev)
    def _():
        for src in range(nc):
            part_wait(src, 1)

    for src in range(nc):
        total += arrive[nc + src].astype(F32)

    con_new = node_update(
        cf[...], total * (1.0 / math.sqrt(size * slots)), cw1[...], cbias[...], cw2[...], cw3[...], cgain[...], cshift[...])
    conbuf[...] = con_new
    con_out[...] = con_new
    window[cut] = con_new

    def win_send(d, back):
        to = lax.rem(cut + d, nc)
        return pltpu.make_async_remote_copy(
            src_ref=conbuf, dst_ref=window.at[back * nc + cut],
            send_sem=wsend.at[back * nc + d], recv_sem=wrecv.at[back * nc + cut],
            device_id=(band - back, to), device_id_type=MESH)

    def win_wait(src, back):
        pltpu.make_async_remote_copy(
            src_ref=conbuf, dst_ref=window.at[back * nc + src],
            send_sem=wsend.at[0], recv_sem=wrecv.at[back * nc + src],
            device_id=(band, cut), device_id_type=MESH).wait_recv()

    @pl.when(has_prev)
    def _():
        for d in range(nc):
            win_send(d, 1).start()

    for d in range(1, nc):
        win_send(d, 0).start()

    lax.fori_loop(pairs // 4, pairs // 2, pair_up, 0)

    @pl.when(has_next)
    def _():
        for d in range(nc):
            part_send(d, 1).wait_send()

    for d in range(1, nc):
        part_send(d, 0).wait_send()
        win_wait(lax.rem(cut + d, nc), 0)

    @pl.when(has_next)
    def _():
        for src in range(nc):
            win_wait(src, 1)

    def row_block(r):
        if blocks == 1:
            return window[r]
        return window[r // blocks, pl.ds(pl.multiple_of(r % blocks * size, size), size)]

    def back(k, carry):
        for u in range(BACK):
            at = k * BACK + u
            right = jnp.concatenate([row_block(order_s[6, 2 * at]), row_block(order_s[6, 2 * at + 1])], axis=0)
            term = jnp.dot(paired[at], right, preferred_element_type=F32)
            carry = carry * order_s[7, at].astype(F32) + term
            scan[at] = carry
        return carry

    lax.fori_loop(0, pairs // BACK, back, jnp.zeros(scan.shape[1:], F32))

    scale = 1.0 / math.sqrt(4 * size)
    def out_copy(i):
        piece = pl.ds(i * STEP, STEP)
        return pltpu.make_async_copy(result.at[piece], var_out.at[piece], out_sem.at[i])

    def update(i, _):
        for u in range(0, STEP, 2):
            c = i * STEP + u
            feats = jnp.concatenate([feat[c], feat[c + 1]], axis=0)
            aggs = [scan[order_s[8, c + e]] * (order_s[9, c + e].astype(F32) * scale) for e in range(2)]
            new = node_update(
                feats, jnp.concatenate(aggs, axis=0),
                vw1[...], vbias[...], vw2[...], vw3[...], vgain[...], vshift[...])
            result[c] = new[:size]
            result[c + 1] = new[size:]
        out_copy(i).start()
        return 0

    lax.fori_loop(0, cols // STEP, update, 0)

    @pl.when(has_prev)
    def _():
        for d in range(nc):
            win_send(d, 1).wait_send()

    for d in range(1, nc):
        win_send(d, 0).wait_send()

    def finish(i, _):
        out_copy(i).wait()
        return 0

    lax.fori_loop(0, cols // STEP, finish, 0)


def on_device(
    nb, nc,
    var_feat, con_feat, slot_column_block, slot_constraint_block, block_count, incidence_coefficients,
    con_first, con_bias, con_second, con_third, con_gain, con_shift,
    var_first, var_bias, var_second, var_third, var_gain, var_shift,
):
    width = var_feat.shape[1]
    slots = slot_column_block.shape[0]
    size = incidence_coefficients.shape[1]
    cols = var_feat.shape[0] // size
    rows = con_feat.shape[0]
    rblocks = 2 * nc * (rows // size)
    fpairs = -(-(slots + rblocks) // (2 * FORWARD)) * FORWARD
    pairs = -(-(slots + cols) // (2 * BACK)) * BACK
    lanes = -(-max(2 * pairs, 2 * fpairs, slots) // 128) * 128
    chunks = slots // CHUNK
    dims = (nb, nc, slots, size, cols, fpairs, pairs, lanes, chunks)
    smem = pl.BlockSpec(memory_space=pltpu.SMEM)
    vmem = pl.BlockSpec(memory_space=pltpu.VMEM)
    hbm = pl.BlockSpec(memory_space=pl.ANY)
    row = lambda v: v.reshape(1, -1)
    con_new, var_new = pl.pallas_call(
        functools.partial(kernel, dims),
        out_shape=(
            jax.ShapeDtypeStruct(con_feat.shape, BF16),
            jax.ShapeDtypeStruct((cols, size, width), BF16),
        ),
        in_specs=[smem, smem, vmem, vmem, smem, hbm, vmem, hbm] + [vmem] * 12,
        out_specs=(vmem, hbm),
        scratch_shapes=[
            pltpu.VMEM((slots, size, size), jnp.int32),
            pltpu.VMEM((slots + 1, size, size), BF16),
            pltpu.VMEM((max(fpairs, pairs), size, width), F32),
            pltpu.VMEM((pairs, size, 2 * size), BF16),
            pltpu.VMEM((cols, size, width), BF16),
            pltpu.VMEM((cols, size, width), BF16),
            pltpu.VMEM((2 * nc, rows, width), BF16),
            pltpu.VMEM((2 * nc, rows, width), BF16),
            pltpu.VMEM((2 * nc, rows, width), BF16),
            pltpu.VMEM((rows, width), BF16),
            pltpu.VMEM((16, lanes), jnp.int32),
            pltpu.SMEM((16, lanes), jnp.int32),
            pltpu.SemaphoreType.DMA((chunks,)),
            pltpu.SemaphoreType.DMA,
            pltpu.SemaphoreType.DMA,
            pltpu.SemaphoreType.DMA((cols // STEP,)),
            pltpu.SemaphoreType.DMA((2 * nc,)),
            pltpu.SemaphoreType.DMA((2 * nc,)),
            pltpu.SemaphoreType.DMA((2 * nc,)),
            pltpu.SemaphoreType.DMA((2 * nc,)),
        ],
        compiler_params=pltpu.CompilerParams(
            collective_id=0, has_side_effects=True, vmem_limit_bytes=63 * 1024 * 1024),
        name="layer",
    )(
        slot_column_block, slot_constraint_block, row(slot_column_block), row(slot_constraint_block), block_count,
        var_feat.reshape(cols, size, width), con_feat, incidence_coefficients,
        con_first, row(con_bias), con_second, con_third, row(con_gain), row(con_shift),
        var_first, row(var_bias), var_second, var_third, row(var_gain), row(var_shift),
    )
    return con_new, var_new.reshape(var_feat.shape)


def solution(mesh):
    both = P(("band", "cuts"))
    wide = P(("band", "cuts"), None)
    in_specs = (wide, wide, both, both, both, P(("band", "cuts"), None, None)) + (P(),) * 12
    body = functools.partial(on_device, mesh.shape["band"], mesh.shape["cuts"])
    return jax.shard_map(body, mesh=mesh, in_specs=in_specs, out_specs=(wide, wide), check_vma=False)
```

```python
import functools
import math

import jax
import jax.numpy as jnp
from jax import lax
from jax.experimental import pallas as pl
from jax.experimental.pallas import tpu as pltpu
from jax.sharding import PartitionSpec as P

EPS = 1e-05
F32 = jnp.float32
BF16 = jnp.bfloat16
MESH = pl.DeviceIdType.MESH
CHUNK = 16
UNROLL = 8
FORWARD = 11
BACK = 20
STEP = 8
SUB = 8


def layer_norm(values, gain, offset):
    center = values - jnp.mean(values, axis=-1, keepdims=True)
    spread = jnp.mean(center * center, axis=-1, keepdims=True)
    return center * lax.rsqrt(spread + EPS) * gain + offset


def node_update(feats, scaled_agg, w_first, bias, w_second, w_third, gain, offset):
    joined = jnp.concatenate([feats, scaled_agg.astype(BF16)], axis=1)
    hidden = jnp.maximum(jnp.dot(joined, w_first, preferred_element_type=F32) + bias, 0.0).astype(BF16)
    middle = jnp.maximum(jnp.dot(hidden, w_second, preferred_element_type=F32), 0.0).astype(BF16)
    output = jnp.dot(middle, w_third, preferred_element_type=F32)
    return layer_norm(feats.astype(F32) + output, gain, offset).astype(BF16)


def order_rows(key_row, key_col, other_col, live_row, live_col, lanes, low, start):
    slots = key_col.shape[0]
    iota = lambda shape, axis: lax.broadcasted_iota(jnp.int32, shape, axis)
    lane = iota((slots, lanes), 1)
    before = (key_row == key_col) & (iota((slots, slots), 1) < iota((slots, slots), 0))
    within = jnp.sum(jnp.where(before, live_row, 0), axis=1, keepdims=True)
    counts = jnp.sum(jnp.where(lane == key_col, live_col, 0), axis=0, keepdims=True)
    counts_col = jnp.sum(jnp.where(iota((lanes, slots), 0) == key_row, live_row, 0), axis=1, keepdims=True)
    steps, steps_col = (counts + 1) >> 1, (counts_col + 1) >> 1
    floor = jnp.where(key_col >= low, low, 0)
    chosen = (lane < key_col) & (lane >= floor)
    base_col = jnp.sum(jnp.where(chosen, steps, 0), axis=1, keepdims=True) + jnp.where(key_col >= low, start, 0)
    place = jnp.where(live_col > 0, base_col * 2 + within, -1)
    hit = place == lane
    index = jnp.sum(jnp.where(hit, iota((slots, lanes), 0) - slots, 0), axis=0, keepdims=True) + slots
    other = jnp.sum(jnp.where(hit, other_col, 0), axis=0, keepdims=True)
    opens = (place == lane * 2) & (within == 0)
    carry = 1 - jnp.sum(jnp.where(opens, 1, 0), axis=0, keepdims=True)
    above, below = iota((lanes, lanes), 0), iota((lanes, lanes), 1)
    upto = (above <= below) & ((above >= low) == (below >= low))
    ends = jnp.sum(jnp.where(upto, steps_col, 0), axis=0, keepdims=True)
    ends += jnp.where(iota((1, lanes), 1) >= low, start, 0)
    last = jnp.maximum(ends - 1, 0)
    filled = jnp.where(counts > 0, 1, 0)
    return [index, other, carry, last, filled]


def kernel(
    dims,
    cb_s, rb_s, cb_v, rb_v, count_s,
    vf_hbm, cf, coef_hbm,
    cw1, cbias, cw2, cw3, cgain, cshift,
    vw1, vbias, vw2, vw3, vgain, vshift,
    con_out, var_out,
    raw, half, scan, paired, feat, result, part, arrive, window, conbuf,
    order_v, order_s,
    raw_sem, feat_sem, order_sem, out_sem, psend, precv, wsend, wrecv,
):
    nb, nc, slots, size, cols, fpairs, pairs, lanes, chunks = dims
    band = lax.axis_index("band")
    cut = lax.axis_index("cuts")
    has_next = band < nb - 1
    has_prev = band > 0

    feat_copy = pltpu.make_async_copy(vf_hbm, feat, feat_sem)
    feat_copy.start()

    def raw_copy(i):
        piece = pl.ds(i * CHUNK, CHUNK)
        return pltpu.make_async_copy(coef_hbm.at[piece], raw.at[piece], raw_sem.at[i])

    for i in range(chunks):
        raw_copy(i).start()

    barrier = pltpu.get_barrier_semaphore()
    for d in range(1, nc):
        pl.semaphore_signal(barrier, inc=1, device_id=(band, lax.rem(cut + d, nc)), device_id_type=MESH)

    @pl.when(has_next)
    def _():
        for d in range(nc):
            pl.semaphore_signal(barrier, inc=1, device_id=(band + 1, lax.rem(cut + d, nc)), device_id_type=MESH)

    @pl.when(has_prev)
    def _():
        for d in range(nc):
            pl.semaphore_signal(barrier, inc=1, device_id=(band - 1, lax.rem(cut + d, nc)), device_id_type=MESH)

    row_c = cb_v[...]
    row_r = rb_v[...]
    diagonal = lax.broadcasted_iota(jnp.int32, (slots, slots), 0) == lax.broadcasted_iota(jnp.int32, (slots, slots), 1)
    col_c = jnp.sum(jnp.where(diagonal, row_c, 0), axis=1, keepdims=True)
    col_r = jnp.sum(jnp.where(diagonal, row_r, 0), axis=1, keepdims=True)
    count = count_s[0]
    early = chunks // 2 * CHUNK
    live_row = jnp.where(lax.broadcasted_iota(jnp.int32, (1, slots), 1) < count, 1, 0)
    live_col = jnp.where(lax.broadcasted_iota(jnp.int32, (slots, 1), 0) < count, 1, 0)
    keys = 2 * nc * (part.shape[1] // size)
    late_row = jnp.where(lax.broadcasted_iota(jnp.int32, (1, slots), 1) >= early, keys, 0)
    late_col = jnp.where(lax.broadcasted_iota(jnp.int32, (slots, 1), 0) >= early, keys, 0)
    rows = order_rows(row_r + late_row, col_r + late_col, col_c, live_row, live_col, lanes, keys, fpairs // 2)
    rows += order_rows(row_c, col_c, col_r, live_row, live_col, lanes, lanes, 0)
    rows += [jnp.zeros((1, lanes), jnp.int32)] * (16 - len(rows))
    order_v[...] = jnp.concatenate(rows, axis=0)
    order_copy = pltpu.make_async_copy(order_v, order_s, order_sem)
    order_copy.start()

    half[slots] = jnp.zeros((size, size), BF16)

    @pl.when(jnp.logical_not(has_prev))
    def _():
        arrive[pl.ds(nc, nc)] = jnp.zeros((nc,) + arrive.shape[1:], BF16)

    @pl.when(jnp.logical_not(has_next))
    def _():
        window[pl.ds(nc, nc)] = jnp.zeros((nc,) + window.shape[1:], BF16)

    def convert(i, _):
        raw_copy(i).wait()

        def some(j, _):
            for u in range(UNROLL):
                at = i * CHUNK + j * UNROLL + u
                half[at] = raw[at].astype(F32).astype(BF16)
            return 0

        lax.fori_loop(0, CHUNK // UNROLL, some, 0)
        return 0

    lax.fori_loop(0, chunks // 2, convert, 0)
    feat_copy.wait()
    order_copy.wait()

    def forward(k, carry):
        for u in range(FORWARD):
            at = k * FORWARD + u
            left = jnp.concatenate([half[order_s[0, 2 * at]], half[order_s[0, 2 * at + 1]]], axis=1)
            right = jnp.concatenate([feat[order_s[1, 2 * at]], feat[order_s[1, 2 * at + 1]]], axis=0)
            term = jnp.dot(left, right, preferred_element_type=F32)
            carry = carry * order_s[2, at].astype(F32) + term
            scan[at] = carry
        return carry

    turns = fpairs // FORWARD
    carry = lax.fori_loop(0, turns // 2, forward, jnp.zeros(scan.shape[1:], F32))
    lax.fori_loop(chunks // 2, chunks, convert, 0)
    lax.fori_loop(turns // 2, turns, forward, carry)

    blocks = part.shape[1] // size

    def fill(q):
        for e in range(blocks):
            r = q * blocks + e
            sums = scan[order_s[3, r]] * order_s[4, r].astype(F32)
            sums += scan[order_s[3, keys + r]] * order_s[4, keys + r].astype(F32)
            part[q, e * size : (e + 1) * size] = sums.astype(BF16)

    def part_send(d, ahead):
        to = lax.rem(cut + d, nc)
        q = ahead * nc + d
        return pltpu.make_async_remote_copy(
            src_ref=part.at[ahead * nc + to], dst_ref=arrive.at[ahead * nc + cut],
            send_sem=psend.at[q], recv_sem=precv.at[ahead * nc + cut],
            device_id=(band + ahead, to), device_id_type=MESH)

    def part_wait(src, ahead):
        pltpu.make_async_remote_copy(
            src_ref=part.at[0], dst_ref=arrive.at[ahead * nc + src],
            send_sem=psend.at[0], recv_sem=precv.at[ahead * nc + src],
            device_id=(band, cut), device_id_type=MESH).wait_recv()

    for q in range(2 * nc):
        fill(q)

    expected = (nc - 1) + jnp.where(has_next, nc, 0) + jnp.where(has_prev, nc, 0)
    pl.semaphore_wait(barrier, expected)

    @pl.when(has_next)
    def _():
        for d in range(nc):
            part_send(d, 1).start()

    for d in range(1, nc):
        part_send(d, 0).start()

    def pair_up(p, _):
        for u in range(2):
            k = p * 2 + u
            left = half[order_s[5, 2 * k]].T
            right = half[order_s[5, 2 * k + 1]].T
            paired[k, :, :size] = left
            paired[k, :, size:] = right
        return 0

    lax.fori_loop(0, pairs // 4, pair_up, 0)

    total = part[cut].astype(F32)
    for d in range(1, nc):
        src = lax.rem(cut + d, nc)
        part_wait(src, 0)
        total += arrive[src].astype(F32)

    @pl.when(has_prev)
    def _():
        for src in range(nc):
            part_wait(src, 1)

    for src in range(nc):
        total += arrive[nc + src].astype(F32)

    con_new = node_update(
        cf[...], total * (1.0 / math.sqrt(size * slots)), cw1[...], cbias[...], cw2[...], cw3[...], cgain[...], cshift[...])
    conbuf[...] = con_new
    con_out[...] = con_new
    window[cut] = con_new

    def win_send(d, back):
        to = lax.rem(cut + d, nc)
        return pltpu.make_async_remote_copy(
            src_ref=conbuf, dst_ref=window.at[back * nc + cut],
            send_sem=wsend.at[back * nc + d], recv_sem=wrecv.at[back * nc + cut],
            device_id=(band - back, to), device_id_type=MESH)

    def win_wait(src, back):
        pltpu.make_async_remote_copy(
            src_ref=conbuf, dst_ref=window.at[back * nc + src],
            send_sem=wsend.at[0], recv_sem=wrecv.at[back * nc + src],
            device_id=(band, cut), device_id_type=MESH).wait_recv()

    @pl.when(has_prev)
    def _():
        for d in range(nc):
            win_send(d, 1).start()

    for d in range(1, nc):
        win_send(d, 0).start()

    lax.fori_loop(pairs // 4, pairs // 2, pair_up, 0)

    @pl.when(has_next)
    def _():
        for d in range(nc):
            part_send(d, 1).wait_send()

    for d in range(1, nc):
        part_send(d, 0).wait_send()
        win_wait(lax.rem(cut + d, nc), 0)

    @pl.when(has_next)
    def _():
        for src in range(nc):
            win_wait(src, 1)

    def row_block(r):
        if blocks == 1:
            return window[r]
        return window[r // blocks, pl.ds(pl.multiple_of(r % blocks * size, size), size)]

    def back(k, carry):
        for u in range(BACK):
            at = k * BACK + u
            right = jnp.concatenate([row_block(order_s[6, 2 * at]), row_block(order_s[6, 2 * at + 1])], axis=0)
            term = jnp.dot(paired[at], right, preferred_element_type=F32)
            carry = carry * order_s[7, at].astype(F32) + term
            scan[at] = carry
        return carry

    lax.fori_loop(0, pairs // BACK, back, jnp.zeros(scan.shape[1:], F32))

    scale = 1.0 / math.sqrt(4 * size)
    def out_copy(i):
        piece = pl.ds(i * STEP, STEP)
        return pltpu.make_async_copy(result.at[piece], var_out.at[piece], out_sem.at[i])

    def update(i, _):
        for u in range(0, STEP, SUB):
            c = i * STEP + u
            feats = feat[pl.ds(c, SUB)].reshape(SUB * size, -1)
            aggs = [scan[order_s[8, c + e]] * (order_s[9, c + e].astype(F32) * scale) for e in range(SUB)]
            new = node_update(
                feats, jnp.concatenate(aggs, axis=0),
                vw1[...], vbias[...], vw2[...], vw3[...], vgain[...], vshift[...])
            result[pl.ds(c, SUB)] = new.reshape(SUB, size, -1)
        out_copy(i).start()
        return 0

    lax.fori_loop(0, cols // STEP, update, 0)

    @pl.when(has_prev)
    def _():
        for d in range(nc):
            win_send(d, 1).wait_send()

    for d in range(1, nc):
        win_send(d, 0).wait_send()

    def finish(i, _):
        out_copy(i).wait()
        return 0

    lax.fori_loop(0, cols // STEP, finish, 0)


def on_device(
    nb, nc,
    var_feat, con_feat, slot_column_block, slot_constraint_block, block_count, incidence_coefficients,
    con_first, con_bias, con_second, con_third, con_gain, con_shift,
    var_first, var_bias, var_second, var_third, var_gain, var_shift,
):
    width = var_feat.shape[1]
    slots = slot_column_block.shape[0]
    size = incidence_coefficients.shape[1]
    cols = var_feat.shape[0] // size
    rows = con_feat.shape[0]
    rblocks = 2 * nc * (rows // size)
    early = slots // CHUNK // 2 * CHUNK
    fpairs = -(-(slots - early + rblocks) // (2 * FORWARD)) * FORWARD * 2
    pairs = -(-(slots + cols) // (2 * BACK)) * BACK
    lanes = -(-max(2 * pairs, 2 * fpairs, 2 * rblocks) // 128) * 128
    chunks = slots // CHUNK
    dims = (nb, nc, slots, size, cols, fpairs, pairs, lanes, chunks)
    smem = pl.BlockSpec(memory_space=pltpu.SMEM)
    vmem = pl.BlockSpec(memory_space=pltpu.VMEM)
    hbm = pl.BlockSpec(memory_space=pl.ANY)
    row = lambda v: v.reshape(1, -1)
    con_new, var_new = pl.pallas_call(
        functools.partial(kernel, dims),
        out_shape=(
            jax.ShapeDtypeStruct(con_feat.shape, BF16),
            jax.ShapeDtypeStruct((cols, size, width), BF16),
        ),
        in_specs=[smem, smem, vmem, vmem, smem, hbm, vmem, hbm] + [vmem] * 12,
        out_specs=(vmem, hbm),
        scratch_shapes=[
            pltpu.VMEM((slots, size, size), jnp.int32),
            pltpu.VMEM((slots + 1, size, size), BF16),
            pltpu.VMEM((max(fpairs, pairs), size, width), F32),
            pltpu.VMEM((pairs, size, 2 * size), BF16),
            pltpu.VMEM((cols, size, width), BF16),
            pltpu.VMEM((cols, size, width), BF16),
            pltpu.VMEM((2 * nc, rows, width), BF16),
            pltpu.VMEM((2 * nc, rows, width), BF16),
            pltpu.VMEM((2 * nc, rows, width), BF16),
            pltpu.VMEM((rows, width), BF16),
            pltpu.VMEM((16, lanes), jnp.int32),
            pltpu.SMEM((16, lanes), jnp.int32),
            pltpu.SemaphoreType.DMA((chunks,)),
            pltpu.SemaphoreType.DMA,
            pltpu.SemaphoreType.DMA,
            pltpu.SemaphoreType.DMA((cols // STEP,)),
            pltpu.SemaphoreType.DMA((2 * nc,)),
            pltpu.SemaphoreType.DMA((2 * nc,)),
            pltpu.SemaphoreType.DMA((2 * nc,)),
            pltpu.SemaphoreType.DMA((2 * nc,)),
        ],
        compiler_params=pltpu.CompilerParams(
            collective_id=0, has_side_effects=True, vmem_limit_bytes=63 * 1024 * 1024),
        name="layer",
    )(
        slot_column_block, slot_constraint_block, row(slot_column_block), row(slot_constraint_block), block_count,
        var_feat.reshape(cols, size, width), con_feat, incidence_coefficients,
        con_first, row(con_bias), con_second, con_third, row(con_gain), row(con_shift),
        var_first, row(var_bias), var_second, var_third, row(var_gain), row(var_shift),
    )
    return con_new, var_new.reshape(var_feat.shape)


def solution(mesh):
    both = P(("band", "cuts"))
    wide = P(("band", "cuts"), None)
    in_specs = (wide, wide, both, both, both, P(("band", "cuts"), None, None)) + (P(),) * 12
    body = functools.partial(on_device, mesh.shape["band"], mesh.shape["cuts"])
    return jax.shard_map(body, mesh=mesh, in_specs=in_specs, out_specs=(wide, wide), check_vma=False)
```

```python
import functools
import math

import jax
import jax.numpy as jnp
from jax import lax
from jax.experimental import pallas as pl
from jax.experimental.pallas import tpu as pltpu
from jax.sharding import PartitionSpec as P

EPS = 1e-05
F32 = jnp.float32
BF16 = jnp.bfloat16
MESH = pl.DeviceIdType.MESH
CHUNK = 16
UNROLL = 8
FORWARD = 22
BACK = 25
STEP = 20
SUB = 20


def layer_norm(values, gain, offset):
    center = values - jnp.mean(values, axis=-1, keepdims=True)
    spread = jnp.mean(center * center, axis=-1, keepdims=True)
    return center * lax.rsqrt(spread + EPS) * gain + offset


def node_update(feats, scaled_agg, w_first, bias, w_second, w_third, gain, offset):
    joined = jnp.concatenate([feats, scaled_agg.astype(BF16)], axis=1)
    hidden = jnp.maximum(jnp.dot(joined, w_first, preferred_element_type=F32) + bias, 0.0).astype(BF16)
    middle = jnp.maximum(jnp.dot(hidden, w_second, preferred_element_type=F32), 0.0).astype(BF16)
    output = jnp.dot(middle, w_third, preferred_element_type=F32)
    return layer_norm(feats.astype(F32) + output, gain, offset).astype(BF16)


def order_rows(key_row, key_col, other_col, live_row, live_col, lanes, low, start):
    slots = key_col.shape[0]
    iota = lambda shape, axis: lax.broadcasted_iota(jnp.int32, shape, axis)
    lane = iota((slots, lanes), 1)
    before = (key_row == key_col) & (iota((slots, slots), 1) < iota((slots, slots), 0))
    within = jnp.sum(jnp.where(before, live_row, 0), axis=1, keepdims=True)
    counts = jnp.sum(jnp.where(lane == key_col, live_col, 0), axis=0, keepdims=True)
    counts_col = jnp.sum(jnp.where(iota((lanes, slots), 0) == key_row, live_row, 0), axis=1, keepdims=True)
    steps, steps_col = (counts + 1) >> 1, (counts_col + 1) >> 1
    floor = jnp.where(key_col >= low, low, 0)
    chosen = (lane < key_col) & (lane >= floor)
    base_col = jnp.sum(jnp.where(chosen, steps, 0), axis=1, keepdims=True) + jnp.where(key_col >= low, start, 0)
    place = jnp.where(live_col > 0, base_col * 2 + within, -1)
    hit = place == lane
    index = jnp.sum(jnp.where(hit, iota((slots, lanes), 0) - slots, 0), axis=0, keepdims=True) + slots
    other = jnp.sum(jnp.where(hit, other_col, 0), axis=0, keepdims=True)
    opens = (place == lane * 2) & (within == 0)
    carry = 1 - jnp.sum(jnp.where(opens, 1, 0), axis=0, keepdims=True)
    above, below = iota((lanes, lanes), 0), iota((lanes, lanes), 1)
    upto = (above <= below) & ((above >= low) == (below >= low))
    ends = jnp.sum(jnp.where(upto, steps_col, 0), axis=0, keepdims=True)
    ends += jnp.where(iota((1, lanes), 1) >= low, start, 0)
    last = jnp.maximum(ends - 1, 0)
    filled = jnp.where(counts > 0, 1, 0)
    return [index, other, carry, last, filled]


def kernel(
    dims,
    cb_s, rb_s, cb_v, rb_v, count_s,
    vf_hbm, cf, coef_hbm,
    cw1, cbias, cw2, cw3, cgain, cshift,
    vw1, vbias, vw2, vw3, vgain, vshift,
    con_out, var_out,
    raw, half, scan, paired, feat, result, part, arrive, window, conbuf,
    order_v, order_s,
    raw_sem, feat_sem, order_sem, out_sem, psend, precv, wsend, wrecv,
):
    nb, nc, slots, size, cols, fpairs, pairs, lanes, chunks = dims
    band = lax.axis_index("band")
    cut = lax.axis_index("cuts")
    has_next = band < nb - 1
    has_prev = band > 0

    feat_copy = pltpu.make_async_copy(vf_hbm, feat, feat_sem)
    feat_copy.start()

    def raw_copy(i):
        piece = pl.ds(i * CHUNK, CHUNK)
        return pltpu.make_async_copy(coef_hbm.at[piece], raw.at[piece], raw_sem.at[i])

    for i in range(chunks):
        raw_copy(i).start()

    barrier = pltpu.get_barrier_semaphore()
    for d in range(1, nc):
        pl.semaphore_signal(barrier, inc=1, device_id=(band, lax.rem(cut + d, nc)), device_id_type=MESH)

    @pl.when(has_next)
    def _():
        for d in range(nc):
            pl.semaphore_signal(barrier, inc=1, device_id=(band + 1, lax.rem(cut + d, nc)), device_id_type=MESH)

    @pl.when(has_prev)
    def _():
        for d in range(nc):
            pl.semaphore_signal(barrier, inc=1, device_id=(band - 1, lax.rem(cut + d, nc)), device_id_type=MESH)

    row_c = cb_v[...]
    row_r = rb_v[...]
    diagonal = lax.broadcasted_iota(jnp.int32, (slots, slots), 0) == lax.broadcasted_iota(jnp.int32, (slots, slots), 1)
    col_c = jnp.sum(jnp.where(diagonal, row_c, 0), axis=1, keepdims=True)
    col_r = jnp.sum(jnp.where(diagonal, row_r, 0), axis=1, keepdims=True)
    count = count_s[0]
    early = chunks // 2 * CHUNK
    live_row = jnp.where(lax.broadcasted_iota(jnp.int32, (1, slots), 1) < count, 1, 0)
    live_col = jnp.where(lax.broadcasted_iota(jnp.int32, (slots, 1), 0) < count, 1, 0)
    keys = 2 * nc * (part.shape[1] // size)
    late_row = jnp.where(lax.broadcasted_iota(jnp.int32, (1, slots), 1) >= early, keys, 0)
    late_col = jnp.where(lax.broadcasted_iota(jnp.int32, (slots, 1), 0) >= early, keys, 0)
    rows = order_rows(row_r + late_row, col_r + late_col, col_c, live_row, live_col, lanes, keys, fpairs // 2)
    rows += order_rows(row_c, col_c, col_r, live_row, live_col, lanes, lanes, 0)
    rows += [jnp.zeros((1, lanes), jnp.int32)] * (16 - len(rows))
    order_v[...] = jnp.concatenate(rows, axis=0)
    order_copy = pltpu.make_async_copy(order_v, order_s, order_sem)
    order_copy.start()

    half[slots] = jnp.zeros((size, size), BF16)

    @pl.when(jnp.logical_not(has_prev))
    def _():
        arrive[pl.ds(nc, nc)] = jnp.zeros((nc,) + arrive.shape[1:], BF16)

    @pl.when(jnp.logical_not(has_next))
    def _():
        window[pl.ds(nc, nc)] = jnp.zeros((nc,) + window.shape[1:], BF16)

    def convert(i, _):
        raw_copy(i).wait()

        def some(j, _):
            for u in range(UNROLL):
                at = i * CHUNK + j * UNROLL + u
                half[at] = raw[at].astype(F32).astype(BF16)
            return 0

        lax.fori_loop(0, CHUNK // UNROLL, some, 0)
        return 0

    lax.fori_loop(0, chunks // 2, convert, 0)
    feat_copy.wait()
    order_copy.wait()

    def forward(k, carry):
        for u in range(FORWARD):
            at = k * FORWARD + u
            left = jnp.concatenate([half[order_s[0, 2 * at]], half[order_s[0, 2 * at + 1]]], axis=1)
            right = jnp.concatenate([feat[order_s[1, 2 * at]], feat[order_s[1, 2 * at + 1]]], axis=0)
            term = jnp.dot(left, right, preferred_element_type=F32)
            carry = carry * order_s[2, at].astype(F32) + term
            scan[at] = carry
        return carry

    turns = fpairs // FORWARD
    carry = lax.fori_loop(0, turns // 2, forward, jnp.zeros(scan.shape[1:], F32))
    lax.fori_loop(chunks // 2, chunks, convert, 0)
    lax.fori_loop(turns // 2, turns, forward, carry)

    blocks = part.shape[1] // size

    def fill(q):
        for e in range(blocks):
            r = q * blocks + e
            sums = scan[order_s[3, r]] * order_s[4, r].astype(F32)
            sums += scan[order_s[3, keys + r]] * order_s[4, keys + r].astype(F32)
            part[q, e * size : (e + 1) * size] = sums.astype(BF16)

    def part_send(d, ahead):
        to = lax.rem(cut + d, nc)
        q = ahead * nc + d
        return pltpu.make_async_remote_copy(
            src_ref=part.at[ahead * nc + to], dst_ref=arrive.at[ahead * nc + cut],
            send_sem=psend.at[q], recv_sem=precv.at[ahead * nc + cut],
            device_id=(band + ahead, to), device_id_type=MESH)

    def part_wait(src, ahead):
        pltpu.make_async_remote_copy(
            src_ref=part.at[0], dst_ref=arrive.at[ahead * nc + src],
            send_sem=psend.at[0], recv_sem=precv.at[ahead * nc + src],
            device_id=(band, cut), device_id_type=MESH).wait_recv()

    for q in range(2 * nc):
        fill(q)

    expected = (nc - 1) + jnp.where(has_next, nc, 0) + jnp.where(has_prev, nc, 0)
    pl.semaphore_wait(barrier, expected)

    @pl.when(has_next)
    def _():
        for d in range(nc):
            part_send(d, 1).start()

    for d in range(1, nc):
        part_send(d, 0).start()

    def pair_up(p, _):
        for u in range(2):
            k = p * 2 + u
            left = half[order_s[5, 2 * k]].T
            right = half[order_s[5, 2 * k + 1]].T
            paired[k, :, :size] = left
            paired[k, :, size:] = right
        return 0

    lax.fori_loop(0, pairs // 4, pair_up, 0)

    total = part[cut].astype(F32)
    for d in range(1, nc):
        src = lax.rem(cut + d, nc)
        part_wait(src, 0)
        total += arrive[src].astype(F32)

    @pl.when(has_prev)
    def _():
        for src in range(nc):
            part_wait(src, 1)

    for src in range(nc):
        total += arrive[nc + src].astype(F32)

    con_new = node_update(
        cf[...], total * (1.0 / math.sqrt(size * slots)), cw1[...], cbias[...], cw2[...], cw3[...], cgain[...], cshift[...])
    conbuf[...] = con_new
    con_out[...] = con_new
    window[cut] = con_new

    def win_send(d, back):
        to = lax.rem(cut + d, nc)
        return pltpu.make_async_remote_copy(
            src_ref=conbuf, dst_ref=window.at[back * nc + cut],
            send_sem=wsend.at[back * nc + d], recv_sem=wrecv.at[back * nc + cut],
            device_id=(band - back, to), device_id_type=MESH)

    def win_wait(src, back):
        pltpu.make_async_remote_copy(
            src_ref=conbuf, dst_ref=window.at[back * nc + src],
            send_sem=wsend.at[0], recv_sem=wrecv.at[back * nc + src],
            device_id=(band, cut), device_id_type=MESH).wait_recv()

    @pl.when(has_prev)
    def _():
        for d in range(nc):
            win_send(d, 1).start()

    for d in range(1, nc):
        win_send(d, 0).start()

    lax.fori_loop(pairs // 4, pairs // 2, pair_up, 0)

    @pl.when(has_next)
    def _():
        for d in range(nc):
            part_send(d, 1).wait_send()

    for d in range(1, nc):
        part_send(d, 0).wait_send()
        win_wait(lax.rem(cut + d, nc), 0)

    @pl.when(has_next)
    def _():
        for src in range(nc):
            win_wait(src, 1)

    def row_block(r):
        if blocks == 1:
            return window[r]
        return window[r // blocks, pl.ds(pl.multiple_of(r % blocks * size, size), size)]

    def back(k, carry):
        for u in range(BACK):
            at = k * BACK + u
            right = jnp.concatenate([row_block(order_s[6, 2 * at]), row_block(order_s[6, 2 * at + 1])], axis=0)
            term = jnp.dot(paired[at], right, preferred_element_type=F32)
            carry = carry * order_s[7, at].astype(F32) + term
            scan[at] = carry
        return carry

    lax.fori_loop(0, pairs // BACK, back, jnp.zeros(scan.shape[1:], F32))

    scale = 1.0 / math.sqrt(4 * size)
    def out_copy(i):
        piece = pl.ds(i * STEP, STEP)
        return pltpu.make_async_copy(result.at[piece], var_out.at[piece], out_sem.at[i])

    def update(i, _):
        for u in range(0, STEP, SUB):
            c = i * STEP + u
            feats = feat[pl.ds(c, SUB)].reshape(SUB * size, -1)
            aggs = [scan[order_s[8, c + e]] * (order_s[9, c + e].astype(F32) * scale) for e in range(SUB)]
            new = node_update(
                feats, jnp.concatenate(aggs, axis=0),
                vw1[...], vbias[...], vw2[...], vw3[...], vgain[...], vshift[...])
            result[pl.ds(c, SUB)] = new.reshape(SUB, size, -1)
        out_copy(i).start()
        return 0

    lax.fori_loop(0, cols // STEP, update, 0)

    @pl.when(has_prev)
    def _():
        for d in range(nc):
            win_send(d, 1).wait_send()

    for d in range(1, nc):
        win_send(d, 0).wait_send()

    def finish(i, _):
        out_copy(i).wait()
        return 0

    lax.fori_loop(0, cols // STEP, finish, 0)


def on_device(
    nb, nc,
    var_feat, con_feat, slot_column_block, slot_constraint_block, block_count, incidence_coefficients,
    con_first, con_bias, con_second, con_third, con_gain, con_shift,
    var_first, var_bias, var_second, var_third, var_gain, var_shift,
):
    width = var_feat.shape[1]
    slots = slot_column_block.shape[0]
    size = incidence_coefficients.shape[1]
    cols = var_feat.shape[0] // size
    rows = con_feat.shape[0]
    rblocks = 2 * nc * (rows // size)
    early = slots // CHUNK // 2 * CHUNK
    fpairs = -(-(slots - early + rblocks) // (2 * FORWARD)) * FORWARD * 2
    pairs = -(-(slots + cols) // (2 * BACK)) * BACK
    lanes = -(-max(2 * pairs, 2 * fpairs, 2 * rblocks) // 128) * 128
    chunks = slots // CHUNK
    dims = (nb, nc, slots, size, cols, fpairs, pairs, lanes, chunks)
    smem = pl.BlockSpec(memory_space=pltpu.SMEM)
    vmem = pl.BlockSpec(memory_space=pltpu.VMEM)
    hbm = pl.BlockSpec(memory_space=pl.ANY)
    row = lambda v: v.reshape(1, -1)
    con_new, var_new = pl.pallas_call(
        functools.partial(kernel, dims),
        out_shape=(
            jax.ShapeDtypeStruct(con_feat.shape, BF16),
            jax.ShapeDtypeStruct((cols, size, width), BF16),
        ),
        in_specs=[smem, smem, vmem, vmem, smem, hbm, vmem, hbm] + [vmem] * 12,
        out_specs=(vmem, hbm),
        scratch_shapes=[
            pltpu.VMEM((slots, size, size), jnp.int32),
            pltpu.VMEM((slots + 1, size, size), BF16),
            pltpu.VMEM((max(fpairs, pairs), size, width), F32),
            pltpu.VMEM((pairs, size, 2 * size), BF16),
            pltpu.VMEM((cols, size, width), BF16),
            pltpu.VMEM((cols, size, width), BF16),
            pltpu.VMEM((2 * nc, rows, width), BF16),
            pltpu.VMEM((2 * nc, rows, width), BF16),
            pltpu.VMEM((2 * nc, rows, width), BF16),
            pltpu.VMEM((rows, width), BF16),
            pltpu.VMEM((16, lanes), jnp.int32),
            pltpu.SMEM((16, lanes), jnp.int32),
            pltpu.SemaphoreType.DMA((chunks,)),
            pltpu.SemaphoreType.DMA,
            pltpu.SemaphoreType.DMA,
            pltpu.SemaphoreType.DMA((cols // STEP,)),
            pltpu.SemaphoreType.DMA((2 * nc,)),
            pltpu.SemaphoreType.DMA((2 * nc,)),
            pltpu.SemaphoreType.DMA((2 * nc,)),
            pltpu.SemaphoreType.DMA((2 * nc,)),
        ],
        compiler_params=pltpu.CompilerParams(
            collective_id=0, has_side_effects=True, vmem_limit_bytes=63 * 1024 * 1024),
        name="layer",
    )(
        slot_column_block, slot_constraint_block, row(slot_column_block), row(slot_constraint_block), block_count,
        var_feat.reshape(cols, size, width), con_feat, incidence_coefficients,
        con_first, row(con_bias), con_second, con_third, row(con_gain), row(con_shift),
        var_first, row(var_bias), var_second, var_third, row(var_gain), row(var_shift),
    )
    return con_new, var_new.reshape(var_feat.shape)


def solution(mesh):
    both = P(("band", "cuts"))
    wide = P(("band", "cuts"), None)
    in_specs = (wide, wide, both, both, both, P(("band", "cuts"), None, None)) + (P(),) * 12
    body = functools.partial(on_device, mesh.shape["band"], mesh.shape["cuts"])
    return jax.shard_map(body, mesh=mesh, in_specs=in_specs, out_specs=(wide, wide), check_vma=False)
```

```python
import functools
import math

import jax
import jax.numpy as jnp
from jax import lax
from jax.experimental import pallas as pl
from jax.experimental.pallas import tpu as pltpu
from jax.sharding import PartitionSpec as P

EPS = 1e-05
F32 = jnp.float32
BF16 = jnp.bfloat16
MESH = pl.DeviceIdType.MESH
CHUNK = 16
UNROLL = 8
FORWARD = 22
BACK = 25
STEP = 10
GATHER = 8


def layer_norm(values, gain, offset):
    center = values - jnp.mean(values, axis=-1, keepdims=True)
    spread = jnp.mean(center * center, axis=-1, keepdims=True)
    return center * lax.rsqrt(spread + EPS) * gain + offset


def node_update(feats, scaled_agg, w_first, bias, w_second, w_third, gain, offset):
    joined = jnp.concatenate([feats, scaled_agg.astype(BF16)], axis=1)
    hidden = jnp.maximum(jnp.dot(joined, w_first, preferred_element_type=F32) + bias, 0.0).astype(BF16)
    middle = jnp.maximum(jnp.dot(hidden, w_second, preferred_element_type=F32), 0.0).astype(BF16)
    output = jnp.dot(middle, w_third, preferred_element_type=F32)
    return layer_norm(feats.astype(F32) + output, gain, offset).astype(BF16)


def order_rows(key_row, key_col, other_col, live_row, live_col, lanes, low, start):
    slots = key_col.shape[0]
    iota = lambda shape, axis: lax.broadcasted_iota(jnp.int32, shape, axis)
    lane = iota((slots, lanes), 1)
    before = (key_row == key_col) & (iota((slots, slots), 1) < iota((slots, slots), 0))
    within = jnp.sum(jnp.where(before, live_row, 0), axis=1, keepdims=True)
    counts = jnp.sum(jnp.where(lane == key_col, live_col, 0), axis=0, keepdims=True)
    counts_col = jnp.sum(jnp.where(iota((lanes, slots), 0) == key_row, live_row, 0), axis=1, keepdims=True)
    steps, steps_col = (counts + 1) >> 1, (counts_col + 1) >> 1
    floor = jnp.where(key_col >= low, low, 0)
    chosen = (lane < key_col) & (lane >= floor)
    base_col = jnp.sum(jnp.where(chosen, steps, 0), axis=1, keepdims=True) + jnp.where(key_col >= low, start, 0)
    place = jnp.where(live_col > 0, base_col * 2 + within, -1)
    hit = place == lane
    index = jnp.sum(jnp.where(hit, iota((slots, lanes), 0) - slots, 0), axis=0, keepdims=True) + slots
    other = jnp.sum(jnp.where(hit, other_col, 0), axis=0, keepdims=True)
    opens = (place == lane * 2) & (within == 0)
    carry = 1 - jnp.sum(jnp.where(opens, 1, 0), axis=0, keepdims=True)
    above, below = iota((lanes, lanes), 0), iota((lanes, lanes), 1)
    upto = (above <= below) & ((above >= low) == (below >= low))
    ends = jnp.sum(jnp.where(upto, steps_col, 0), axis=0, keepdims=True)
    ends += jnp.where(iota((1, lanes), 1) >= low, start, 0)
    last = jnp.maximum(ends - 1, 0)
    filled = jnp.where(counts > 0, 1, 0)
    return [index, other, carry, last, filled]


def kernel(
    dims,
    cb_s, rb_s, cb_v, rb_v, count_s,
    vf_hbm, cf, coef_hbm,
    cw1, cbias, cw2, cw3, cgain, cshift,
    con_out, agg_out,
    raw, half, scan, paired, feat, result, part, arrive, window, conbuf,
    order_v, order_s,
    raw_sem, feat_sem, order_sem, out_sem, psend, precv, wsend, wrecv,
):
    nb, nc, slots, size, cols, fpairs, pairs, lanes, chunks = dims
    band = lax.axis_index("band")
    cut = lax.axis_index("cuts")
    has_next = band < nb - 1
    has_prev = band > 0

    feat_copy = pltpu.make_async_copy(vf_hbm, feat, feat_sem)
    feat_copy.start()

    def raw_copy(i):
        piece = pl.ds(i * CHUNK, CHUNK)
        return pltpu.make_async_copy(coef_hbm.at[piece], raw.at[piece], raw_sem.at[i])

    for i in range(chunks):
        raw_copy(i).start()

    barrier = pltpu.get_barrier_semaphore()
    for d in range(1, nc):
        pl.semaphore_signal(barrier, inc=1, device_id=(band, lax.rem(cut + d, nc)), device_id_type=MESH)

    @pl.when(has_next)
    def _():
        for d in range(nc):
            pl.semaphore_signal(barrier, inc=1, device_id=(band + 1, lax.rem(cut + d, nc)), device_id_type=MESH)

    @pl.when(has_prev)
    def _():
        for d in range(nc):
            pl.semaphore_signal(barrier, inc=1, device_id=(band - 1, lax.rem(cut + d, nc)), device_id_type=MESH)

    row_c = cb_v[...]
    row_r = rb_v[...]
    diagonal = lax.broadcasted_iota(jnp.int32, (slots, slots), 0) == lax.broadcasted_iota(jnp.int32, (slots, slots), 1)
    col_c = jnp.sum(jnp.where(diagonal, row_c, 0), axis=1, keepdims=True)
    col_r = jnp.sum(jnp.where(diagonal, row_r, 0), axis=1, keepdims=True)
    count = count_s[0]
    early = chunks // 2 * CHUNK
    live_row = jnp.where(lax.broadcasted_iota(jnp.int32, (1, slots), 1) < count, 1, 0)
    live_col = jnp.where(lax.broadcasted_iota(jnp.int32, (slots, 1), 0) < count, 1, 0)
    keys = 2 * nc * (part.shape[1] // size)
    late_row = jnp.where(lax.broadcasted_iota(jnp.int32, (1, slots), 1) >= early, keys, 0)
    late_col = jnp.where(lax.broadcasted_iota(jnp.int32, (slots, 1), 0) >= early, keys, 0)
    rows = order_rows(row_r + late_row, col_r + late_col, col_c, live_row, live_col, lanes, keys, fpairs // 2)
    rows += order_rows(row_c, col_c, col_r, live_row, live_col, lanes, lanes, 0)
    rows += [jnp.zeros((1, lanes), jnp.int32)] * (16 - len(rows))
    order_v[...] = jnp.concatenate(rows, axis=0)
    order_copy = pltpu.make_async_copy(order_v, order_s, order_sem)
    order_copy.start()

    half[slots] = jnp.zeros((size, size), BF16)

    @pl.when(jnp.logical_not(has_prev))
    def _():
        arrive[pl.ds(nc, nc)] = jnp.zeros((nc,) + arrive.shape[1:], BF16)

    @pl.when(jnp.logical_not(has_next))
    def _():
        window[pl.ds(nc, nc)] = jnp.zeros((nc,) + window.shape[1:], BF16)

    def convert(i, _):
        raw_copy(i).wait()

        def some(j, _):
            for u in range(UNROLL):
                at = i * CHUNK + j * UNROLL + u
                half[at] = raw[at].astype(F32).astype(BF16)
            return 0

        lax.fori_loop(0, CHUNK // UNROLL, some, 0)
        return 0

    lax.fori_loop(0, chunks // 2, convert, 0)
    feat_copy.wait()
    order_copy.wait()

    def forward(k, carry):
        for u in range(FORWARD):
            at = k * FORWARD + u
            left = jnp.concatenate([half[order_s[0, 2 * at]], half[order_s[0, 2 * at + 1]]], axis=1)
            right = jnp.concatenate([feat[order_s[1, 2 * at]], feat[order_s[1, 2 * at + 1]]], axis=0)
            term = jnp.dot(left, right, preferred_element_type=F32)
            carry = carry * order_s[2, at].astype(F32) + term
            scan[at] = carry
        return carry

    turns = fpairs // FORWARD
    carry = lax.fori_loop(0, turns // 2, forward, jnp.zeros(scan.shape[1:], F32))
    lax.fori_loop(chunks // 2, chunks, convert, 0)
    lax.fori_loop(turns // 2, turns, forward, carry)

    blocks = part.shape[1] // size

    def fill(q):
        for e in range(blocks):
            r = q * blocks + e
            sums = scan[order_s[3, r]] * order_s[4, r].astype(F32)
            sums += scan[order_s[3, keys + r]] * order_s[4, keys + r].astype(F32)
            part[q, e * size : (e + 1) * size] = sums.astype(BF16)

    def part_send(d, ahead):
        to = lax.rem(cut + d, nc)
        q = ahead * nc + d
        return pltpu.make_async_remote_copy(
            src_ref=part.at[ahead * nc + to], dst_ref=arrive.at[ahead * nc + cut],
            send_sem=psend.at[q], recv_sem=precv.at[ahead * nc + cut],
            device_id=(band + ahead, to), device_id_type=MESH)

    def part_wait(src, ahead):
        pltpu.make_async_remote_copy(
            src_ref=part.at[0], dst_ref=arrive.at[ahead * nc + src],
            send_sem=psend.at[0], recv_sem=precv.at[ahead * nc + src],
            device_id=(band, cut), device_id_type=MESH).wait_recv()

    for q in range(2 * nc):
        fill(q)

    expected = (nc - 1) + jnp.where(has_next, nc, 0) + jnp.where(has_prev, nc, 0)
    pl.semaphore_wait(barrier, expected)

    @pl.when(has_next)
    def _():
        for d in range(nc):
            part_send(d, 1).start()

    for d in range(1, nc):
        part_send(d, 0).start()

    def pair_up(p, _):
        for u in range(2):
            k = p * 2 + u
            left = half[order_s[5, 2 * k]].T
            right = half[order_s[5, 2 * k + 1]].T
            paired[k, :, :size] = left
            paired[k, :, size:] = right
        return 0

    lax.fori_loop(0, pairs // 4, pair_up, 0)

    total = part[cut].astype(F32)
    for d in range(1, nc):
        src = lax.rem(cut + d, nc)
        part_wait(src, 0)
        total += arrive[src].astype(F32)

    @pl.when(has_prev)
    def _():
        for src in range(nc):
            part_wait(src, 1)

    for src in range(nc):
        total += arrive[nc + src].astype(F32)

    con_new = node_update(
        cf[...], total * (1.0 / math.sqrt(size * slots)), cw1[...], cbias[...], cw2[...], cw3[...], cgain[...], cshift[...])
    conbuf[...] = con_new
    con_out[...] = con_new
    window[cut] = con_new

    def win_send(d, back):
        to = lax.rem(cut + d, nc)
        return pltpu.make_async_remote_copy(
            src_ref=conbuf, dst_ref=window.at[back * nc + cut],
            send_sem=wsend.at[back * nc + d], recv_sem=wrecv.at[back * nc + cut],
            device_id=(band - back, to), device_id_type=MESH)

    def win_wait(src, back):
        pltpu.make_async_remote_copy(
            src_ref=conbuf, dst_ref=window.at[back * nc + src],
            send_sem=wsend.at[0], recv_sem=wrecv.at[back * nc + src],
            device_id=(band, cut), device_id_type=MESH).wait_recv()

    @pl.when(has_prev)
    def _():
        for d in range(nc):
            win_send(d, 1).start()

    for d in range(1, nc):
        win_send(d, 0).start()

    lax.fori_loop(pairs // 4, pairs // 2, pair_up, 0)

    @pl.when(has_next)
    def _():
        for d in range(nc):
            part_send(d, 1).wait_send()

    for d in range(1, nc):
        part_send(d, 0).wait_send()
        win_wait(lax.rem(cut + d, nc), 0)

    @pl.when(has_next)
    def _():
        for src in range(nc):
            win_wait(src, 1)

    def row_block(r):
        if blocks == 1:
            return window[r]
        return window[r // blocks, pl.ds(pl.multiple_of(r % blocks * size, size), size)]

    def back(k, carry):
        for u in range(BACK):
            at = k * BACK + u
            right = jnp.concatenate([row_block(order_s[6, 2 * at]), row_block(order_s[6, 2 * at + 1])], axis=0)
            term = jnp.dot(paired[at], right, preferred_element_type=F32)
            carry = carry * order_s[7, at].astype(F32) + term
            scan[at] = carry
        return carry

    lax.fori_loop(0, pairs // BACK, back, jnp.zeros(scan.shape[1:], F32))

    scale = 1.0 / math.sqrt(4 * size)
    def out_copy(i):
        piece = pl.ds(i * GATHER, GATHER)
        return pltpu.make_async_copy(result.at[piece], agg_out.at[piece], out_sem.at[i])

    def gather(i, _):
        for u in range(GATHER):
            c = i * GATHER + u
            result[c] = (scan[order_s[8, c]] * (order_s[9, c].astype(F32) * scale)).astype(BF16)
        out_copy(i).start()
        return 0

    lax.fori_loop(0, cols // GATHER, gather, 0)

    @pl.when(has_prev)
    def _():
        for d in range(nc):
            win_send(d, 1).wait_send()

    for d in range(1, nc):
        win_send(d, 0).wait_send()

    def finish(i, _):
        out_copy(i).wait()
        return 0

    lax.fori_loop(0, cols // GATHER, finish, 0)


def column_kernel(feat, agg, con, vw1, vbias, vw2, vw3, vgain, vshift, con_out, var_out):
    @pl.when(pl.program_id(0) == 0)
    def _():
        con_out[...] = con[...]

    var_out[...] = node_update(
        feat[...], agg[...], vw1[...], vbias[...], vw2[...], vw3[...], vgain[...], vshift[...])


def on_device(
    nb, nc,
    var_feat, con_feat, slot_column_block, slot_constraint_block, block_count, incidence_coefficients,
    con_first, con_bias, con_second, con_third, con_gain, con_shift,
    var_first, var_bias, var_second, var_third, var_gain, var_shift,
):
    width = var_feat.shape[1]
    slots = slot_column_block.shape[0]
    size = incidence_coefficients.shape[1]
    cols = var_feat.shape[0] // size
    rows = con_feat.shape[0]
    rblocks = 2 * nc * (rows // size)
    early = slots // CHUNK // 2 * CHUNK
    fpairs = -(-(slots - early + rblocks) // (2 * FORWARD)) * FORWARD * 2
    pairs = -(-(slots + cols) // (2 * BACK)) * BACK
    lanes = -(-max(2 * pairs, 2 * fpairs, 2 * rblocks) // 128) * 128
    chunks = slots // CHUNK
    dims = (nb, nc, slots, size, cols, fpairs, pairs, lanes, chunks)
    smem = pl.BlockSpec(memory_space=pltpu.SMEM)
    vmem = pl.BlockSpec(memory_space=pltpu.VMEM)
    hbm = pl.BlockSpec(memory_space=pl.ANY)
    row = lambda v: v.reshape(1, -1)
    con_new, agg = pl.pallas_call(
        functools.partial(kernel, dims),
        out_shape=(
            jax.ShapeDtypeStruct(con_feat.shape, BF16),
            jax.ShapeDtypeStruct((cols, size, width), BF16),
        ),
        in_specs=[smem, smem, vmem, vmem, smem, hbm, vmem, hbm] + [vmem] * 6,
        out_specs=(vmem, hbm),
        scratch_shapes=[
            pltpu.VMEM((slots, size, size), jnp.int32),
            pltpu.VMEM((slots + 1, size, size), BF16),
            pltpu.VMEM((max(fpairs, pairs), size, width), F32),
            pltpu.VMEM((pairs, size, 2 * size), BF16),
            pltpu.VMEM((cols, size, width), BF16),
            pltpu.VMEM((cols, size, width), BF16),
            pltpu.VMEM((2 * nc, rows, width), BF16),
            pltpu.VMEM((2 * nc, rows, width), BF16),
            pltpu.VMEM((2 * nc, rows, width), BF16),
            pltpu.VMEM((rows, width), BF16),
            pltpu.VMEM((16, lanes), jnp.int32),
            pltpu.SMEM((16, lanes), jnp.int32),
            pltpu.SemaphoreType.DMA((chunks,)),
            pltpu.SemaphoreType.DMA,
            pltpu.SemaphoreType.DMA,
            pltpu.SemaphoreType.DMA((cols // GATHER,)),
            pltpu.SemaphoreType.DMA((2 * nc,)),
            pltpu.SemaphoreType.DMA((2 * nc,)),
            pltpu.SemaphoreType.DMA((2 * nc,)),
            pltpu.SemaphoreType.DMA((2 * nc,)),
        ],
        compiler_params=pltpu.CompilerParams(
            collective_id=0, has_side_effects=True, vmem_limit_bytes=63 * 1024 * 1024),
        name="layer",
    )(
        slot_column_block, slot_constraint_block, row(slot_column_block), row(slot_constraint_block), block_count,
        var_feat.reshape(cols, size, width), con_feat, incidence_coefficients,
        con_first, row(con_bias), con_second, con_third, row(con_gain), row(con_shift),
    )
    weights = (var_first, row(var_bias), var_second, var_third, row(var_gain), row(var_shift))
    moving = pl.BlockSpec((STEP * size, width), lambda i: (i, 0))
    still = lambda v: pl.BlockSpec(v.shape, lambda i: (0, 0))
    return pl.pallas_call(
        column_kernel,
        grid=(cols // STEP,),
        out_shape=(
            jax.ShapeDtypeStruct(con_feat.shape, BF16),
            jax.ShapeDtypeStruct(var_feat.shape, BF16),
        ),
        in_specs=[moving, moving, still(con_new)] + [still(w) for w in weights],
        out_specs=(still(con_new), moving),
        compiler_params=pltpu.CompilerParams(vmem_limit_bytes=63 * 1024 * 1024),
        name="columns",
    )(var_feat, agg.reshape(var_feat.shape), con_new, *weights)


def solution(mesh):
    both = P(("band", "cuts"))
    wide = P(("band", "cuts"), None)
    in_specs = (wide, wide, both, both, both, P(("band", "cuts"), None, None)) + (P(),) * 12
    body = functools.partial(on_device, mesh.shape["band"], mesh.shape["cuts"])
    return jax.shard_map(body, mesh=mesh, in_specs=in_specs, out_specs=(wide, wide), check_vma=False)
```
